128 devices in a mesh: ctx: 32 (over y, z, core), head: 4 (over x).
Axes of the slice: x: 4, y: 4, z: 4, core: 2. Of those that a mesh axis runs over, the one named last changes fastest.
Arguments:
- entries: bfloat16 [65536, 2048], P('ctx', 'head'), may hold values from -6 to 6
- gating: bfloat16 [65536, 2048], P('ctx', 'head'), may hold values from -6 to 6
- state_in: bfloat16 [65536, 128], P('ctx'), may hold values from -2 to 2
- state_out: bfloat16 [65536, 128], P('ctx'), may hold values from -2 to 2
- step_size: float32 [32, 65536], P('head', 'ctx'), may hold values from 0.2 to 1.5
- decay_rate: float32 [32], P('head'), may hold values from 1.5258789e-06 to 0.1
- skip_gain: float32 [32], P('head'), may hold values from 0.5 to 1.5
- level_gate: float32 [32, 5, 65536], P('head', None, 'ctx'), may hold values from 0.2 to 1.5
- norm_gain: float32 [2048], P('head'), may hold values from 0.5 to 1.5
- cotangent: bfloat16 [65536, 2048], P('ctx'), may hold values from -0.119628906 to 0.119628906
- master_weight: float32 [2048, 2048], P('ctx', 'head'), may hold values from -0.125 to 0.125
- first_moment: float32 [2048, 2048], P('ctx', 'head'), may hold values from -3 to 3
- second_moment: float32 [2048, 2048], P('ctx', 'head'), may hold values from 0.1 to 10
Outputs:
- normed: bfloat16 [65536, 2048], P('ctx', 'head')
- weights: bfloat16 [2048, 2048], P(None, 'head')
- gradient: float32 [2048, 2048], P('ctx', 'head')
The draws below stay inside these ranges and needn't reach their ends.
All inputs are finite; a program needn't handle non-finite values.
Results may differ from the reference program's by a relative error of at most 0.0059.
Values may be sent and summed in bfloat16 or wider, within the bound.
A program may use at most 128 MiB of HBM per device.

```python
import math
import jax
import jax.numpy as jnp
from jax import lax

D = 2048
HEADS = 32
HEAD_DIM = 64
STATE = 128
TOK_DEV = 2048
BLOCK = 256
LEVELS = 5
INNER = 2048
TOKENS = 65536
N_CTX = 32


def block_scale(key, extent, shards, least, top_value):
    def one(axis_at, blocks):
        steps = jax.random.uniform(jax.random.fold_in(jax.random.fold_in(key, 6), axis_at), (blocks,), jnp.float32, least / len(shards), top_value / len(shards))
        return jnp.repeat(jnp.exp(steps), extent[axis_at] // blocks).reshape((-1,) + (1,) * (len(extent) - axis_at - 1))

    gain = one(*shards[0])
    for cut in shards[1:]:
        gain = gain * one(*cut)
    return gain


def gaussian(key, extent, spread, limit, split=(), kind=jnp.bfloat16):
    factor_of = block_scale(key, extent, split, -0.22, 0.18) if split else 1.0
    drawn = jax.random.normal(key, extent, jnp.float32) * spread * factor_of
    return jnp.minimum(jnp.maximum(drawn, -limit), limit).astype(kind)


def setup_inputs(seed: int = 0) -> dict:
    arg_keys = jax.random.split(jax.random.key(seed), 14)
    return {
        "entries": gaussian(arg_keys[0], (TOKENS, INNER), 1.0, 6.0, ((0, 32), (1, 4))),
        "gating": gaussian(arg_keys[1], (TOKENS, INNER), 1.0, 6.0, ((0, 32), (1, 4))),
        "state_in": gaussian(arg_keys[2], (TOKENS, STATE), 0.3, 2.0, ((0, 32),)),
        "state_out": gaussian(arg_keys[3], (TOKENS, STATE), 0.3, 2.0, ((0, 32),)),
        "step_size": jnp.clip(0.2 + 1.3 * jax.random.uniform(arg_keys[4], (HEADS, TOKENS), jnp.float32) ** block_scale(arg_keys[4], (HEADS, TOKENS), ((0, 4), (1, 32)), -0.2, 0.2), 0.2, 1.5),
        "decay_rate": jnp.clip(jnp.exp(math.log(0.1) - 11.090355 * jax.random.uniform(arg_keys[5], (HEADS,), jnp.float32) ** block_scale(arg_keys[5], (HEADS,), ((0, 4),), -0.2, 0.2)), 1.5258789289873675e-06, 0.1),
        "skip_gain": jnp.clip(0.5 + 1.0 * jax.random.uniform(arg_keys[6], (HEADS,), jnp.float32) ** block_scale(arg_keys[6], (HEADS,), ((0, 4),), -0.2, 0.2), 0.5, 1.5),
        "level_gate": jnp.clip(0.2 + 1.3 * jax.random.uniform(arg_keys[7], (HEADS, LEVELS, TOKENS), jnp.float32) ** block_scale(arg_keys[7], (HEADS, LEVELS, TOKENS), ((0, 4), (2, 32)), -0.2, 0.2), 0.2, 1.5),
        "norm_gain": jnp.clip(1.0 + 0.1 * jax.random.normal(arg_keys[8], (INNER,), jnp.float32), 0.5, 1.5),
        "cotangent": gaussian(arg_keys[9], (TOKENS, D), 0.02, 0.119628906, ((0, 32),)),
        "master_weight": gaussian(arg_keys[10], (D, INNER), INNER ** -0.5, 0.125, ((0, 32), (1, 4)), jnp.float32),
        "first_moment": gaussian(arg_keys[11], (D, INNER), 0.5, 3.0, ((0, 32), (1, 4)), jnp.float32),
        "second_moment": jnp.clip(jnp.exp(math.log(10.0) - 4.6051702 * jax.random.uniform(arg_keys[12], (D, INNER), jnp.float32) ** block_scale(arg_keys[12], (D, INNER), ((0, 32), (1, 4)), -0.2, 0.2)), 0.1, 10.0),
    }


def rounded(values):
    return lax.optimization_barrier(values.astype(jnp.bfloat16)).astype(jnp.float32)

def block_scan(scaled, state_in, state_out, log_decay):
    length, head_count, head_width = scaled.shape
    state_width = state_in.shape[1]
    blocks = length // BLOCK
    decay_blocks = log_decay.reshape(head_count, blocks, BLOCK).transpose(1, 0, 2)
    value_blocks = scaled.reshape(blocks, BLOCK, head_count, head_width)
    in_blocks = state_in.reshape(blocks, BLOCK, state_width)
    out_blocks = state_out.reshape(blocks, BLOCK, state_width)
    causal = jnp.arange(BLOCK)[:, None] >= jnp.arange(BLOCK)[None, :]

    def advance(running, pieces):
        decays, value_block, in_block, out_block = pieces
        prefix = jnp.cumsum(decays, axis=-1)
        scores = jnp.dot(out_block, in_block.T, preferred_element_type=jnp.float32)
        gap_matrix = jnp.where(causal[None], prefix[:, :, None] - prefix[:, None, :], 0.0)
        decay_mask = jnp.where(causal[None], jnp.exp(gap_matrix), 0.0)
        mix = (scores[None] * decay_mask).astype(jnp.bfloat16)
        within = jnp.einsum('hts,shp->thp', mix.astype(jnp.float32), value_block.astype(jnp.float32))
        carried = jnp.einsum('tn,hpn->thp', out_block.astype(jnp.float32), rounded(running))
        carried = carried * jnp.exp(prefix).T[:, :, None]
        to_end = (value_block.astype(jnp.float32) * jnp.exp(prefix[:, -1:] - prefix).T[:, :, None]).astype(jnp.bfloat16)
        update = jnp.einsum('thp,tn->hpn', to_end.astype(jnp.float32), in_block.astype(jnp.float32))
        running = jnp.exp(prefix[:, -1])[:, None, None] * running + update
        return (running, (within + carried, prefix))
    start = jnp.zeros((head_count, head_width, state_width), jnp.float32)
    end_state, (outputs, prefixes) = lax.scan(advance, start, (decay_blocks, value_blocks, in_blocks, out_blocks))
    totals = prefixes[:, :, -1]
    offsets = jnp.cumsum(totals, axis=0) - totals
    cumulative = (prefixes + offsets[:, :, None]).transpose(1, 0, 2).reshape(head_count, length)
    return (outputs.reshape(length, head_count, head_width), end_state, cumulative)

def level_states(all_ends, all_totals, position, depth):
    members = all_ends.shape[0]
    positions = jnp.arange(members, dtype=jnp.int32)
    between = (positions[None, :] > positions[:, None]) & (positions[None, :] < position)
    gap_decay = lax.optimization_barrier(jnp.sum(jnp.where(between[:, :, None], all_totals[None, :, :], 0.0), axis=1))
    collected = []
    for rung in range(depth):
        selected = (positions < position) & (jnp.right_shift(positions, rung + 1) == jnp.right_shift(position, rung + 1))
        selected = selected & (jnp.bitwise_and(jnp.right_shift(position, rung), 1) == 1)
        selected = selected & (jnp.bitwise_and(jnp.right_shift(positions, rung), 1) == 0)
        factor = jnp.where(selected[:, None], jnp.exp(gap_decay), 0.0)
        collected.append(jnp.einsum('jh,jhpn->hpn', factor, all_ends, precision=lax.Precision.HIGHEST))
    return collected

def finish(within, cumulative, by_head, gating, state_out, gate_rows, skip_gain, levels):
    length, head_count, head_width = within.shape
    across = jnp.zeros_like(within)
    for rung, level_state in enumerate(levels):
        readout = jnp.einsum('tn,hpn->thp', state_out.astype(jnp.float32), rounded(level_state))
        across = across + readout * gate_rows[:, rung, :].T[:, :, None]
    mixed = within + across * jnp.exp(cumulative).T[:, :, None] + skip_gain[None, :, None] * by_head.astype(jnp.float32)
    return mixed.reshape(length, head_count * head_width) * jax.nn.silu(gating.astype(jnp.float32))

def adamw(gradient, master, moment_one, moment_two):
    moment_one = 0.9 * moment_one + 0.1 * gradient
    moment_two = 0.95 * moment_two + 0.05 * gradient * gradient
    ratio = moment_one / (1.0 - 0.9 ** 10) / (jnp.sqrt(moment_two / (1.0 - 0.95 ** 10)) + 1e-08)
    return (master - 0.1 * (ratio + 0.1 * master)).astype(jnp.bfloat16)

def reference(entries, gating, state_in, state_out, step_size, decay_rate, skip_gain, level_gate, norm_gain, cotangent, master_weight, first_moment, second_moment):
    members = N_CTX
    depth = members.bit_length() - 1
    seg_entries = entries.reshape(members, TOK_DEV, HEADS, HEAD_DIM)
    seg_in = state_in.reshape(members, TOK_DEV, STATE)
    seg_out = state_out.reshape(members, TOK_DEV, STATE)
    seg_steps = step_size.reshape(HEADS, members, TOK_DEV).transpose(1, 0, 2)

    def local_pass(arrays):
        part_x, part_in, part_out, part_steps = arrays
        log_decay = -decay_rate[:, None] * part_steps
        scaled = (part_x.astype(jnp.float32) * part_steps.T[:, :, None]).astype(jnp.bfloat16)
        return block_scan(scaled, part_in, part_out, log_decay)
    withins, all_ends, cumulatives = lax.map(local_pass, (seg_entries, seg_in, seg_out, seg_steps))
    all_totals = cumulatives[:, :, -1]
    seg_gating = gating.reshape(members, TOK_DEV, INNER)
    seg_gate = level_gate.reshape(HEADS, LEVELS, members, TOK_DEV).transpose(2, 0, 1, 3)

    def output_pass(arrays):
        position, part_within, part_cum, part_x, part_z, part_out, part_gate = arrays
        levels = level_states(all_ends, all_totals, position, depth)
        gated = finish(part_within, part_cum, part_x, part_z, part_out, part_gate, skip_gain, levels)
        mean_sq = lax.optimization_barrier(jnp.sum(gated * gated, axis=1)) / INNER
        return (gated * lax.rsqrt(mean_sq + 1e-05)[:, None] * norm_gain[None, :]).astype(jnp.bfloat16)
    normed = lax.map(output_pass, (jnp.arange(members, dtype=jnp.int32), withins, cumulatives, seg_entries, seg_gating, seg_out, seg_gate))
    normed = normed.reshape(TOKENS, INNER)
    gradient = lax.dot_general(cotangent, normed, (((0,), (0,)), ((), ())), preferred_element_type=jnp.float32)
    weights = adamw(gradient, master_weight, first_moment, second_moment)
    return (normed, weights, gradient)
```

```python
import jax
import jax.numpy as jnp
from jax import lax
from jax.experimental import pallas as pl
from jax.experimental.pallas import tpu as pltpu
from jax.sharding import PartitionSpec as P

HD = 64
BLK = 256
NB = 8
NH = 8
CH = 512
ST = 128
LEV = 5
INNER = 2048
DM = 2048
F32 = jnp.float32
BF16 = jnp.bfloat16
MESH = pl.DeviceIdType.MESH
DIMS = 4


def nt(a, b):
    return lax.dot_general(a, b, (((1,), (1,)), ((), ())), preferred_element_type=F32)


def nn(a, b):
    return lax.dot_general(a, b, (((1,), (0,)), ((), ())), preferred_element_type=F32)


def flip(y, z, mask):
    if mask & 1:
        z = z + 1 - 2 * lax.rem(z, 2)
    if mask & 2:
        z = 3 - z
    if mask & 4:
        y = y + 1 - 2 * lax.rem(y, 2)
    if mask & 8:
        y = 3 - y
    return y, z


def stream_dims(s):
    return [(s + t) % DIMS for t in range(DIMS)]


def span(dims):
    masks = [0]
    for d in dims:
        masks = masks + [m | (1 << d) for m in masks]
    return masks


SCRATCH = dict(
    xv=pltpu.VMEM((NB, BLK, CH), BF16),
    zv=pltpu.VMEM((NB, BLK, CH), BF16),
    bv=pltpu.VMEM((NB, BLK, ST), BF16),
    cv=pltpu.VMEM((NB, BLK, ST), BF16),
    dtv=pltpu.VMEM((NH, NB * BLK), F32),
    gatev=pltpu.VMEM((LEV, NH, NB * BLK), F32),
    ngv=pltpu.VMEM((1, CH), F32),
    gcol=pltpu.VMEM((CH, 128), F32),
    xt=pltpu.VMEM((NB, CH, BLK), BF16),
    xa=pltpu.VMEM((NB, CH, BLK), BF16),
    runs=pltpu.VMEM((NB, CH, ST), BF16),
    run=pltpu.VMEM((CH, ST), F32),
    acc=pltpu.VMEM((NB, CH, BLK), F32),
    sil=pltpu.VMEM((NB, CH, BLK), F32),
    ep=pltpu.VMEM((NB, NH, BLK), F32),
    e1=pltpu.VMEM((NB, NH, BLK), F32),
    ecum=pltpu.VMEM((NB, NH, BLK), F32),
    ebuf=pltpu.VMEM((2, CH, ST), F32),
    dbuf=pltpu.VMEM((2, NH, 128), F32),
    sz=pltpu.VMEM((4, CH // 2, ST), F32),
    dz=pltpu.VMEM((4, NH, 128), F32),
    sy=pltpu.VMEM((4, CH // 2, ST), BF16),
    dy=pltpu.VMEM((4, NH, 128), F32),
    lev=pltpu.VMEM((LEV, CH, ST), BF16),
    fac=pltpu.VMEM((LEV, NH, BLK), F32),
    ssb=pltpu.VMEM((4, NB, 8, BLK), F32),
    nt_=pltpu.VMEM((CH, NB * BLK), BF16),
    cotv=pltpu.VMEM((NB * BLK, DM), BF16),
    gsend=pltpu.VMEM((8, 256, 256), BF16),
    gown=pltpu.VMEM((8, 256, 256), F32),
    grecv=pltpu.VMEM((8, 256, 256), BF16),
    part=pltpu.VMEM((16, 256, 128), F32),
    sb=pltpu.VMEM((4, 15, HD, 128), BF16),
    r0=pltpu.VMEM((4, 8, HD, 128), BF16),
    r1=pltpu.VMEM((4, 4, HD, 128), BF16),
    r2=pltpu.VMEM((4, 2, HD, 128), BF16),
    r3=pltpu.VMEM((4, 1, HD, 128), BF16),
    gt=pltpu.VMEM((128, 256), F32),
    gx=pltpu.VMEM((64, 256), F32),
    mw=pltpu.VMEM((3, 128, 256), F32),
    w=pltpu.VMEM((16, 2, 128, 256), BF16),
    s_x=pltpu.SemaphoreType.DMA((NB,)),
    s_z=pltpu.SemaphoreType.DMA((NB,)),
    s_in=pltpu.SemaphoreType.DMA((6,)),
    s_n=pltpu.SemaphoreType.DMA((NB,)),
    s_out=pltpu.SemaphoreType.DMA((4,)),
    s_m=pltpu.SemaphoreType.DMA((3,)),
    e_s=pltpu.SemaphoreType.DMA((2,)),
    e_r=pltpu.SemaphoreType.DMA((2,)),
    z_s=pltpu.SemaphoreType.DMA((3, 2)),
    z_r=pltpu.SemaphoreType.DMA((3, 2)),
    y_s=pltpu.SemaphoreType.DMA((3, 2)),
    y_r=pltpu.SemaphoreType.DMA((3, 2)),
    l_s=pltpu.SemaphoreType.DMA((4,)),
    l_r=pltpu.SemaphoreType.DMA((4,)),
    q_s=pltpu.SemaphoreType.DMA((NB, 3)),
    q_r=pltpu.SemaphoreType.DMA((NB, 3)),
    m_s=pltpu.SemaphoreType.DMA((3,)),
    m_r=pltpu.SemaphoreType.DMA((3,)),
    p_s=pltpu.SemaphoreType.DMA((8,)),
    p_r=pltpu.SemaphoreType.DMA((8,)),
    r_s=pltpu.SemaphoreType.DMA((4, 15)),
    r_r=pltpu.SemaphoreType.DMA((4, 15)),
    g_s=pltpu.SemaphoreType.DMA((1,)),
    g_r=pltpu.SemaphoreType.DMA((1,)),
    a_s=pltpu.SemaphoreType.DMA((4, 15)),
    a_r=pltpu.SemaphoreType.DMA((4, 15)),
    c_s=pltpu.SemaphoreType.DMA((4, 16)),
    c_r=pltpu.SemaphoreType.DMA((4, 16)),
)


class Refs:
    pass


def kernel(
    x_h, z_h, b_h, c_h, dt_h, dr_s, sk_s, gate_h, ng_h, cot_h, mw_h, m1_h, m2_h,
    n_out, w_out, g_out, *scratch,
):
    v = Refs()
    for name, ref in zip(SCRATCH, scratch):
        setattr(v, name, ref)
    ctx = lax.axis_index("ctx")
    head = lax.axis_index("head")
    core = lax.rem(ctx, 2)
    z = lax.rem(ctx // 2, 4)
    y = ctx // 8
    half = pl.multiple_of(core * 256, 256)
    other = pl.multiple_of((1 - core) * 256, 256)

    def at(yy, zz, cc):
        return ((yy * 4 + zz) * 2 + cc, head)

    partner = at(y, z, 1 - core)
    zpeers = [at(y, lax.rem(z + d, 4), core) for d in (1, 2, 3)]
    ypeers = [at(lax.rem(y + d, 4), z, core) for d in (1, 2, 3)]
    xpeers = [(ctx, lax.rem(head + d, 4)) for d in (1, 2, 3)]
    cube = []
    for d in range(DIMS):
        yy, zz = flip(y, z, 1 << d)
        cube.append(at(yy, zz, core))

    def remote(src, dst, ssem, rsem, dev):
        return pltpu.make_async_remote_copy(
            src_ref=src, dst_ref=dst, send_sem=ssem, recv_sem=rsem, device_id=dev, device_id_type=MESH
        )

    barrier = pltpu.get_barrier_semaphore()
    for dev in [partner] + zpeers + ypeers + xpeers:
        pl.semaphore_signal(barrier, inc=1, device_id=dev, device_id_type=MESH)

    def load_x(b):
        return pltpu.make_async_copy(x_h.at[pl.ds(b * BLK, BLK)], v.xv.at[b], v.s_x.at[b])

    def load_z(b):
        return pltpu.make_async_copy(z_h.at[pl.ds(b * BLK, BLK)], v.zv.at[b], v.s_z.at[b])

    ld_dt = pltpu.make_async_copy(dt_h, v.dtv, v.s_in.at[0])
    ld_b = pltpu.make_async_copy(b_h, v.bv, v.s_in.at[1])
    ld_c = pltpu.make_async_copy(c_h, v.cv, v.s_in.at[2])
    ld_g = pltpu.make_async_copy(gate_h, v.gatev, v.s_in.at[3])
    ld_n = pltpu.make_async_copy(ng_h, v.ngv, v.s_in.at[4])
    ld_cot = pltpu.make_async_copy(cot_h, v.cotv, v.s_in.at[5])
    ld_dt.start()
    load_x(0).start()
    ld_b.start()
    for b in range(1, NB):
        load_x(b).start()
    ld_c.start()
    for b in range(NB):
        load_z(b).start()
    ld_g.start()
    ld_n.start()
    ld_cot.start()
    moments = (mw_h, m1_h, m2_h)
    ld_m = [
        pltpu.make_async_copy(
            ref.at[:, pl.ds(half, 256)],
            v.mw.at[k, pl.ds(pl.multiple_of(core * 64, 64), 64)],
            v.s_m.at[k],
        )
        for k, ref in enumerate(moments)
    ]
    for cp in ld_m:
        cp.start()
    ex_m = [
        remote(
            ref.at[:, pl.ds(other, 256)],
            v.mw.at[k, pl.ds(pl.multiple_of(core * 64, 64), 64)],
            v.m_s.at[k],
            v.m_r.at[k],
            partner,
        )
        for k, ref in enumerate(moments)
    ]

    iota_h = lax.broadcasted_iota(jnp.int32, (NH, 128), 0)
    rate = jnp.zeros((NH, 128), F32)
    for h in range(NH):
        rate = jnp.where(iota_h == h, dr_s[h], rate)
    row = lax.broadcasted_iota(jnp.int32, (BLK, BLK), 0)
    col = lax.broadcasted_iota(jnp.int32, (BLK, BLK), 1)
    upper = (row <= col).astype(F32)
    rate2 = jnp.concatenate([rate, rate], axis=1)
    v.run[...] = jnp.zeros_like(v.run)
    ld_dt.wait()

    def hs(h):
        return slice(h * HD, (h + 1) * HD)

    def a1(b, off):
        dt = v.dtv[:, pl.ds(pl.multiple_of(b * BLK, BLK), BLK)]
        ld = -rate2 * dt
        prefix = lax.dot_general(
            ld, upper, (((1,), (0,)), ((), ())), precision=lax.Precision.HIGHEST, preferred_element_type=F32
        )
        total = jnp.broadcast_to(prefix[:, BLK - 1 :], (NH, BLK))
        tail = jnp.exp(total - prefix)
        v.ep[b] = jnp.exp(prefix)
        v.e1[b] = jnp.exp(prefix - total)
        v.ecum[b] = jnp.exp(off + prefix)
        load_x(b).wait()
        xt = v.xv[b].T
        v.xt[b] = xt
        for h in range(NH):
            scaled = (xt[hs(h)].astype(F32) * dt[h : h + 1]).astype(BF16)
            v.xa[b, hs(h)] = (scaled.astype(F32) * tail[h : h + 1]).astype(BF16)
        upd = nn(v.xa[b], v.bv[b])
        et = jnp.exp(total[:, :128])
        for h in range(NH):
            old = v.run[hs(h)]
            v.runs[b, hs(h)] = old.astype(BF16)
            v.run[hs(h)] = old * et[h : h + 1] + upd[hs(h)]
        return off + total

    ld_b.wait()
    dsum = lax.fori_loop(0, NB, a1, jnp.zeros((NH, BLK), F32))
    v.ebuf[core] = v.run[...]
    v.dbuf[core] = dsum[:, :128]

    pl.semaphore_wait(barrier, 10)
    ex_e = [
        remote(v.ebuf.at[core], v.ebuf.at[core], v.e_s.at[0], v.e_r.at[0], partner),
        remote(v.dbuf.at[core], v.dbuf.at[core], v.e_s.at[1], v.e_r.at[1], partner),
    ]
    for cp in ex_e:
        cp.start()
    for cp in ex_m:
        cp.start()

    ld_c.wait()
    causal = row <= col

    def a2(b, carry):
        c_b = v.cv[b]
        scores = jnp.where(causal, nt(v.bv[b], c_b), 0.0).astype(BF16)
        local = nn(v.xa[b], scores)
        carried = nt(v.runs[b], c_b)
        for h in range(NH):
            v.acc[b, hs(h)] = local[hs(h)] * v.e1[b, h : h + 1] + carried[hs(h)] * v.ep[b, h : h + 1]
        load_z(b).wait()
        zt = v.zv[b].T
        for h in range(NH):
            zz = zt[hs(h)].astype(F32)
            v.sil[b, hs(h)] = zz / (1.0 + jnp.exp(-zz))
        return carry

    lax.fori_loop(0, 2, a2, 0)

    for cp in ex_e:
        cp.wait()
    d0, d1 = v.dbuf[0], v.dbuf[1]
    v.dz[z] = d0 + d1
    dpre = jnp.where(core == 1, d0, 0.0)

    def hrow(ref, k, j):
        return jnp.exp(ref[k, pl.ds(core * 4 + j, 1)])

    for j in range(4):
        rows = pl.ds(pl.multiple_of(half + j * HD, HD), HD)
        v.sz[z, hs(j)] = v.ebuf[0, rows] * hrow(v.dbuf, 1, j) + v.ebuf[1, rows]
    ex_z = []
    for d in range(3):
        ex_z.append(remote(v.sz.at[z], v.sz.at[z], v.z_s.at[d, 0], v.z_r.at[d, 0], zpeers[d]))
        ex_z.append(remote(v.dz.at[z], v.dz.at[z], v.z_s.at[d, 1], v.z_r.at[d, 1], zpeers[d]))
    for cp in ex_z:
        cp.start()
    lax.fori_loop(2, 6, a2, 0)

    for cp in ex_z:
        cp.wait()
    v.dy[y] = (v.dz[0] + v.dz[1]) + (v.dz[2] + v.dz[3])
    zpre = dpre
    for k in range(3):
        zpre = zpre + jnp.where(z > k, v.dz[k], 0.0)
    zflip = z + 1 - 2 * lax.rem(z, 2)
    for j in range(4):
        s01 = v.sz[0, hs(j)] * hrow(v.dz, 1, j) + v.sz[1, hs(j)]
        s012 = s01 * hrow(v.dz, 2, j) + v.sz[2, hs(j)]
        v.sy[y, hs(j)] = (s012 * hrow(v.dz, 3, j) + v.sz[3, hs(j)]).astype(BF16)
        rows = pl.ds(pl.multiple_of(half + j * HD, HD), HD)
        v.lev[1, rows] = v.sz[zflip, hs(j)].astype(BF16)
        v.lev[2, rows] = s01.astype(BF16)
    ex_y = []
    for d in range(3):
        ex_y.append(remote(v.sy.at[y], v.sy.at[y], v.y_s.at[d, 0], v.y_r.at[d, 0], ypeers[d]))
        ex_y.append(remote(v.dy.at[y], v.dy.at[y], v.y_s.at[d, 1], v.y_r.at[d, 1], ypeers[d]))
    for cp in ex_y:
        cp.start()

    def swap(level):
        piece = v.lev.at[level, pl.ds(half, 256)]
        return remote(piece, piece, v.l_s.at[level - 1], v.l_r.at[level - 1], partner)

    for level in (1, 2):
        swap(level).start()
    v.lev[0] = v.ebuf[0].astype(BF16)

    def set_factor(level, value):
        v.fac[level] = jnp.concatenate([value, value], axis=1)

    set_factor(0, jnp.full((NH, 128), jnp.where(core == 1, 1.0, 0.0), F32))
    set_factor(1, jnp.where(lax.rem(z, 2) == 1, jnp.exp(dpre), 0.0))
    set_factor(2, jnp.where(z >= 2, jnp.exp(dpre + jnp.where(z == 3, v.dz[2], 0.0)), 0.0))
    lax.fori_loop(6, 8, a2, 0)
    ld_g.wait()
    for level in (1, 2):
        swap(level).wait()

    def scaled_gate(b, level):
        lanes = pl.ds(pl.multiple_of(b * BLK, BLK), BLK)
        return v.gatev[level, :, lanes] * (v.fac[level] * v.ecum[b])

    def b1(b, carry):
        c_b = v.cv[b]
        reads = [nt(v.lev[level], c_b) for level in range(3)]
        gates = [scaled_gate(b, level) for level in range(3)]
        for h in range(NH):
            add = reads[0][hs(h)] * gates[0][h : h + 1]
            for level in (1, 2):
                add = add + reads[level][hs(h)] * gates[level][h : h + 1]
            v.acc[b, hs(h)] = v.acc[b, hs(h)] + add
        return carry

    lax.fori_loop(0, 5, b1, 0)

    for cp in ex_y:
        cp.wait()
    yflip = y + 1 - 2 * lax.rem(y, 2)
    for j in range(4):
        s01 = v.sy[0, hs(j)].astype(F32) * hrow(v.dy, 1, j) + v.sy[1, hs(j)].astype(F32)
        rows = pl.ds(pl.multiple_of(half + j * HD, HD), HD)
        v.lev[3, rows] = v.sy[yflip, hs(j)]
        v.lev[4, rows] = s01.astype(BF16)
    for level in (3, 4):
        swap(level).start()
    set_factor(3, jnp.where(lax.rem(y, 2) == 1, jnp.exp(zpre), 0.0))
    set_factor(4, jnp.where(y >= 2, jnp.exp(zpre + jnp.where(y == 3, v.dy[2], 0.0)), 0.0))
    lax.fori_loop(5, 8, b1, 0)
    ld_n.wait()
    v.gcol[...] = jnp.broadcast_to(v.ngv[...], (128, CH)).T
    for level in (3, 4):
        swap(level).wait()

    def ex_q(b, d):
        piece = v.ssb.at[head, b]
        return remote(piece, piece, v.q_s.at[b, d], v.q_r.at[b, d], xpeers[d])

    def b2(b, carry):
        c_b = v.cv[b]
        reads = [nt(v.lev[level], c_b) for level in (3, 4)]
        gates = [scaled_gate(b, level) for level in (3, 4)]
        squares = jnp.zeros((8, BLK), F32)
        for h in range(NH):
            inside = v.acc[b, hs(h)] + reads[0][hs(h)] * gates[0][h : h + 1] + reads[1][hs(h)] * gates[1][h : h + 1]
            mixed = inside + v.xt[b, hs(h)].astype(F32) * sk_s[h]
            gated = mixed * v.sil[b, hs(h)]
            v.acc[b, hs(h)] = gated
            squares = squares + jnp.sum((gated * gated).reshape(8, 8, BLK), axis=0)
        v.ssb[head, b] = squares
        for d in range(3):
            ex_q(b, d).start()
        return carry

    def b3(b, carry):
        for d in range(3):
            ex_q(b, d).wait()
        total = (v.ssb[0, b] + v.ssb[1, b]) + (v.ssb[2, b] + v.ssb[3, b])
        r = lax.rsqrt(jnp.sum(total, axis=0, keepdims=True) / INNER + 1e-05)
        lanes = pl.ds(pl.multiple_of(b * BLK, BLK), BLK)
        for h in range(NH):
            gain = v.gcol[hs(h)]
            n = v.acc[b, hs(h)] * r * jnp.concatenate([gain, gain], axis=1)
            v.nt_[hs(h), lanes] = n.astype(BF16)
        v.xv[b] = v.nt_[:, lanes].T
        pltpu.make_async_copy(v.xv.at[b], n_out.at[pl.ds(b * BLK, BLK)], v.s_n.at[b]).start()
        return carry

    lax.fori_loop(0, NB, b2, 0)
    lax.fori_loop(0, NB, b3, 0)

    ld_cot.wait()
    def ex_p(p):
        return remote(v.gsend.at[p], v.grecv.at[p], v.p_s.at[p], v.p_r.at[p], partner)

    recv_bufs = (v.r0, v.r1, v.r2, v.r3)
    starts = (0, 8, 12, 14)

    def sent_masks(s, t):
        dims = stream_dims(s)
        return [m | (1 << dims[t]) for m in span(dims[t + 1 :])]

    def ex_r(s, t, i):
        dims = stream_dims(s)
        k = starts[t] + i
        return remote(v.sb.at[s, k], recv_bufs[t].at[s, i], v.r_s.at[s, k], v.r_r.at[s, k], cube[dims[t]])

    def finish_pair(p):
        ex_p(p).wait()
        for a in range(2):
            lanes = slice(a * 128, (a + 1) * 128)
            m = 2 * p + a
            total = v.gown[p, :, lanes] + v.grecv[p, :, lanes].astype(F32)
            for s in range(4):
                if m >> s & 1:
                    v.sb[s, sent_masks(s, 0).index(m)] = total[hs(s)].astype(BF16)
                else:
                    v.part[m, hs(s)] = total[hs(s)]
        for s in range(4):
            for i, m in enumerate(sent_masks(s, 0)):
                if m >> 1 == p:
                    ex_r(s, 0, i).start()

    for p in range(7, -1, -1):
        sides = []
        for m in (2 * p, 2 * p + 1):
            yy, zz = flip(y, z, m)
            sides.append(v.cotv[:, pl.ds(pl.multiple_of((yy * 4 + zz) * 128, 128), 128)])
        cot = jnp.concatenate(sides, axis=1)
        v.gsend[p] = nn(v.nt_[pl.ds(other, 256), :], cot).astype(BF16)
        ex_p(p).start()
        v.gown[p] = nn(v.nt_[pl.ds(half, 256), :], cot)
        if p < 7:
            finish_pair(p + 1)
    finish_pair(0)

    for t in range(3):
        for s in range(4):
            dims = stream_dims(s)
            kept = span(dims[t + 1 :])
            nxt = sent_masks(s, t + 1)
            for i, m in enumerate(kept):
                ex_r(s, t, i).wait()
                total = v.part[m, hs(s)] + recv_bufs[t][s, i].astype(F32)
                if m in nxt:
                    k = nxt.index(m)
                    v.sb[s, starts[t + 1] + k] = total.astype(BF16)
                    ex_r(s, t + 1, k).start()
                else:
                    v.part[m, hs(s)] = total
    for s in range(4):
        ex_r(s, 3, 0).wait()
        v.gt[:, hs(s)] = (v.part[0, hs(s)] + v.r3[s, 0].astype(F32)).T

    ex_g = remote(
        v.gt.at[pl.ds(pl.multiple_of((1 - core) * 64, 64), 64)], v.gx, v.g_s.at[0], v.g_r.at[0], partner
    )
    ex_g.start()
    for cp in ld_m:
        cp.wait()
    for cp in ex_m:
        cp.wait()
    own = y * 4 + z
    grad = v.gt[...]
    one = 0.9 * v.mw[1] + 0.1 * grad
    two = 0.95 * v.mw[2] + 0.05 * grad * grad
    ratio = one / (1.0 - 0.9**10) / (jnp.sqrt(two / (1.0 - 0.95**10)) + 1e-08)
    master = v.mw[0]
    v.w[own, core] = (master - 0.1 * (ratio + 0.1 * master)).astype(BF16)

    def slot(m):
        yy, zz = flip(y, z, m)
        return yy * 4 + zz

    def ex_a(s, t, i):
        dims = stream_dims(s)
        m = span(dims[:t])[i]
        piece = v.w.at[slot(m), core, pl.ds(s * 32, 32)]
        k = (1 << t) - 1 + i
        return remote(piece, piece, v.a_s.at[s, k], v.a_r.at[s, k], cube[dims[t]])

    def ex_c(s, i):
        m = span(stream_dims(s))[i]
        piece = v.w.at[slot(m), core, pl.ds(s * 32, 32)]
        return remote(piece, piece, v.c_s.at[s, i], v.c_r.at[s, i], partner)

    for t in range(4):
        for s in range(4):
            ex_a(s, t, 0).start()
    for s in range(4):
        ex_c(s, 0).start()
    for t in range(4):
        for i in range(1 << t):
            for s in range(4):
                ex_a(s, t, i).wait_recv()
                got = (1 << t) + i
                for later in range(t + 1, 4):
                    ex_a(s, later, got).start()
                ex_c(s, got).start()
    ex_g.wait()
    mine = pl.ds(pl.multiple_of(core * 64, 64), 64)
    outs = [
        pltpu.make_async_copy(v.gt.at[mine], g_out.at[:, pl.ds(half, 256)], v.s_out.at[0]),
        pltpu.make_async_copy(v.gx, g_out.at[:, pl.ds(other, 256)], v.s_out.at[1]),
        pltpu.make_async_copy(v.w.at[:, core], w_out.at[:, :, pl.ds(half, 256)], v.s_out.at[2]),
    ]
    for cp in outs:
        cp.start()
    for s in range(4):
        for i in range(16):
            ex_c(s, i).wait()
    last = pltpu.make_async_copy(v.w.at[:, 1 - core], w_out.at[:, :, pl.ds(other, 256)], v.s_out.at[3])
    last.start()
    for s in range(4):
        for t in range(4):
            for i in range(1 << t):
                ex_a(s, t, i).wait_send()
    for b in range(NB):
        pltpu.make_async_copy(v.xv.at[b], n_out.at[pl.ds(b * BLK, BLK)], v.s_n.at[b]).wait()
    for cp in outs:
        cp.wait()
    last.wait()


def on_device(
    entries, gating, state_in, state_out, step_size, decay_rate, skip_gain, level_gate,
    norm_gain, cotangent, master_weight, first_moment, second_moment,
):
    anyspace = pl.BlockSpec(memory_space=pl.ANY)
    smem = pl.BlockSpec(memory_space=pltpu.SMEM)
    normed, weights, gradient = pl.pallas_call(
        kernel,
        out_shape=(
            jax.ShapeDtypeStruct((NB * BLK, CH), BF16),
            jax.ShapeDtypeStruct((16, 128, CH), BF16),
            jax.ShapeDtypeStruct((64, CH), F32),
        ),
        in_specs=[anyspace] * 5 + [smem] * 2 + [anyspace] * 6,
        out_specs=(anyspace,) * 3,
        scratch_shapes=list(SCRATCH.values()),
        compiler_params=pltpu.CompilerParams(
            collective_id=0, has_side_effects=True, vmem_limit_bytes=60 * 1024 * 1024
        ),
    )(
        entries,
        gating,
        state_in.reshape(NB, BLK, ST),
        state_out.reshape(NB, BLK, ST),
        step_size,
        decay_rate,
        skip_gain,
        level_gate.transpose(1, 0, 2),
        norm_gain.reshape(1, CH),
        cotangent,
        master_weight,
        first_moment,
        second_moment,
    )
    return normed, weights.reshape(DM, CH), gradient


def solution(mesh):
    return jax.shard_map(
        on_device,
        mesh=mesh,
        in_specs=(
            P("ctx", "head"),
            P("ctx", "head"),
            P("ctx", None),
            P("ctx", None),
            P("head", "ctx"),
            P("head"),
            P("head"),
            P("head", None, "ctx"),
            P("head"),
            P("ctx", None),
            P("ctx", "head"),
            P("ctx", "head"),
            P("ctx", "head"),
        ),
        out_specs=(P("ctx", "head"), P(None, "head"), P("ctx", "head")),
        check_vma=False,
    )
```

```python
import jax
import jax.numpy as jnp
from jax import lax
from jax.experimental import pallas as pl
from jax.experimental.pallas import tpu as pltpu
from jax.sharding import PartitionSpec as P

HD = 64
BLK = 256
NB = 8
NH = 8
CH = 512
ST = 128
LEV = 5
INNER = 2048
DM = 2048
F32 = jnp.float32
BF16 = jnp.bfloat16
MESH = pl.DeviceIdType.MESH
DIMS = 4


def nt(a, b):
    return lax.dot_general(a, b, (((1,), (1,)), ((), ())), preferred_element_type=F32)


def nn(a, b):
    return lax.dot_general(a, b, (((1,), (0,)), ((), ())), preferred_element_type=F32)


def flip(y, z, mask):
    if mask & 1:
        z = z + 1 - 2 * lax.rem(z, 2)
    if mask & 2:
        z = 3 - z
    if mask & 4:
        y = y + 1 - 2 * lax.rem(y, 2)
    if mask & 8:
        y = 3 - y
    return y, z


def stream_dims(s):
    return [(s + t) % DIMS for t in range(DIMS)]


def span(dims):
    masks = [0]
    for d in dims:
        masks = masks + [m | (1 << d) for m in masks]
    return masks


LAG = 2
HOP = 3


def schedule_events():
    out = []
    for s in range(4):
        dims = stream_dims(s)
        sent = {}
        done = {m: 7 - (m >> 1) + LAG for m in range(16)}
        for m in range(16):
            if m >> dims[0] & 1:
                sent[m] = done[m]
        for t in range(3):
            for i, m in enumerate(span(dims[t + 1 :])):
                when = max(sent[m | 1 << dims[t]] + HOP, done[m])
                done[m] = when
                out.append((when, s, t, i))
                if m >> dims[t + 1] & 1:
                    sent[m] = when
    return sorted(out, key=lambda e: (e[0], e[2], e[3], e[1]))


SCRATCH = dict(
    xv=pltpu.VMEM((NB, BLK, CH), BF16),
    pre=pltpu.VMEM((NB, NH, BLK), F32),
    zv=pltpu.VMEM((NB, BLK, CH), BF16),
    bv=pltpu.VMEM((NB, BLK, ST), BF16),
    cv=pltpu.VMEM((NB, BLK, ST), BF16),
    dtv=pltpu.VMEM((NH, NB * BLK), F32),
    gatev=pltpu.VMEM((LEV, NH, NB * BLK), F32),
    ngv=pltpu.VMEM((1, CH), F32),
    gcol=pltpu.VMEM((CH, 128), F32),
    xt=pltpu.VMEM((NB, CH, BLK), BF16),
    xa=pltpu.VMEM((NB, CH, BLK), BF16),
    runs=pltpu.VMEM((NB, CH, ST), BF16),
    run=pltpu.VMEM((CH, ST), F32),
    acc=pltpu.VMEM((NB, CH, BLK), F32),
    sil=pltpu.VMEM((NB, CH, BLK), F32),
    ep=pltpu.VMEM((NB, NH, BLK), F32),
    e1=pltpu.VMEM((NB, NH, BLK), F32),
    ecum=pltpu.VMEM((NB, NH, BLK), F32),
    ebuf=pltpu.VMEM((2, CH, ST), F32),
    dbuf=pltpu.VMEM((2, NH, 128), F32),
    sz=pltpu.VMEM((4, CH // 2, ST), BF16),
    dz=pltpu.VMEM((4, NH, 128), F32),
    sy=pltpu.VMEM((4, CH // 2, ST), BF16),
    dy=pltpu.VMEM((4, NH, 128), F32),
    lev=pltpu.VMEM((LEV, CH, ST), BF16),
    fac=pltpu.VMEM((LEV, NH, BLK), F32),
    ssb=pltpu.VMEM((4, NB, 1, BLK), F32),
    nt_=pltpu.VMEM((CH, NB * BLK), BF16),
    cotv=pltpu.VMEM((NB * BLK, DM), BF16),
    gsend=pltpu.VMEM((8, 256, 256), BF16),
    gown=pltpu.VMEM((8, 256, 256), F32),
    grecv=pltpu.VMEM((8, 256, 256), BF16),
    part=pltpu.VMEM((16, 256, 128), F32),
    sb=pltpu.VMEM((4, 15, HD, 128), BF16),
    r0=pltpu.VMEM((4, 8, HD, 128), BF16),
    r1=pltpu.VMEM((4, 4, HD, 128), BF16),
    r2=pltpu.VMEM((4, 2, HD, 128), BF16),
    r3=pltpu.VMEM((4, 1, HD, 128), BF16),
    gt=pltpu.VMEM((128, 256), F32),
    mw=pltpu.VMEM((3, 128, 256), F32),
    s_x=pltpu.SemaphoreType.DMA((NB,)),
    s_z=pltpu.SemaphoreType.DMA((NB,)),
    s_in=pltpu.SemaphoreType.DMA((6,)),
    s_m=pltpu.SemaphoreType.DMA((3,)),
    e_s=pltpu.SemaphoreType.DMA((2,)),
    e_r=pltpu.SemaphoreType.DMA((2,)),
    z_s=pltpu.SemaphoreType.DMA((3, 2)),
    z_r=pltpu.SemaphoreType.DMA((3, 2)),
    y_s=pltpu.SemaphoreType.DMA((3, 2)),
    y_r=pltpu.SemaphoreType.DMA((3, 2)),
    l_s=pltpu.SemaphoreType.DMA((4,)),
    l_r=pltpu.SemaphoreType.DMA((4,)),
    q_s=pltpu.SemaphoreType.DMA((NB, 3)),
    q_r=pltpu.SemaphoreType.DMA((NB, 3)),
    m_s=pltpu.SemaphoreType.DMA((3,)),
    m_r=pltpu.SemaphoreType.DMA((3,)),
    p_s=pltpu.SemaphoreType.DMA((8,)),
    p_r=pltpu.SemaphoreType.DMA((8,)),
    r_s=pltpu.SemaphoreType.DMA((4, 15)),
    r_r=pltpu.SemaphoreType.DMA((4, 15)),
    g_s=pltpu.SemaphoreType.DMA((1,)),
    g_r=pltpu.SemaphoreType.DMA((1,)),
    a_s=pltpu.SemaphoreType.DMA((4, 15)),
    a_r=pltpu.SemaphoreType.DMA((4, 15)),
    c_s=pltpu.SemaphoreType.DMA((4, 16)),
    c_r=pltpu.SemaphoreType.DMA((4, 16)),
)


class Refs:
    pass


def kernel(
    x_h, z_h, b_h, c_h, dt_h, dr_s, sk_s, gate_h, ng_h, cot_h, mw_h, m1_h, m2_h,
    n_out, w_out, gt_out, gx_out, *scratch,
):
    v = Refs()
    for name, ref in zip(SCRATCH, scratch):
        setattr(v, name, ref)
    v.w, v.gx = w_out, gx_out
    ctx = lax.axis_index("ctx")
    head = lax.axis_index("head")
    core = lax.rem(ctx, 2)
    z = lax.rem(ctx // 2, 4)
    y = ctx // 8
    half = pl.multiple_of(core * 256, 256)
    other = pl.multiple_of((1 - core) * 256, 256)

    def at(yy, zz, cc):
        return ((yy * 4 + zz) * 2 + cc, head)

    partner = at(y, z, 1 - core)
    zpeers = [at(y, lax.rem(z + d, 4), core) for d in (1, 2, 3)]
    ypeers = [at(lax.rem(y + d, 4), z, core) for d in (1, 2, 3)]
    xpeers = [(ctx, lax.rem(head + d, 4)) for d in (1, 2, 3)]
    cube = []
    for d in range(DIMS):
        yy, zz = flip(y, z, 1 << d)
        cube.append(at(yy, zz, core))

    def remote(src, dst, ssem, rsem, dev):
        return pltpu.make_async_remote_copy(
            src_ref=src, dst_ref=dst, send_sem=ssem, recv_sem=rsem, device_id=dev, device_id_type=MESH
        )

    barrier = pltpu.get_barrier_semaphore()
    for dev in [partner] + zpeers + ypeers + xpeers:
        pl.semaphore_signal(barrier, inc=1, device_id=dev, device_id_type=MESH)

    def load_x(b):
        return pltpu.make_async_copy(x_h.at[pl.ds(b * BLK, BLK)], v.xv.at[b], v.s_x.at[b])

    def load_z(b):
        return pltpu.make_async_copy(z_h.at[pl.ds(b * BLK, BLK)], v.zv.at[b], v.s_z.at[b])

    ld_dt = pltpu.make_async_copy(dt_h, v.dtv, v.s_in.at[0])
    ld_b = pltpu.make_async_copy(b_h, v.bv, v.s_in.at[1])
    ld_c = pltpu.make_async_copy(c_h, v.cv, v.s_in.at[2])
    ld_g = pltpu.make_async_copy(gate_h, v.gatev, v.s_in.at[3])
    ld_n = pltpu.make_async_copy(ng_h, v.ngv, v.s_in.at[4])
    ld_cot = pltpu.make_async_copy(cot_h, v.cotv, v.s_in.at[5])
    ld_dt.start()
    load_x(0).start()
    ld_b.start()
    for b in range(1, NB):
        load_x(b).start()
    ld_c.start()
    for b in range(NB):
        load_z(b).start()
    ld_g.start()
    ld_n.start()
    ld_cot.start()
    moments = (mw_h, m1_h, m2_h)
    ld_m = [
        pltpu.make_async_copy(
            ref.at[:, pl.ds(half, 256)],
            v.mw.at[k, pl.ds(pl.multiple_of(core * 64, 64), 64)],
            v.s_m.at[k],
        )
        for k, ref in enumerate(moments)
    ]
    for cp in ld_m:
        cp.start()
    ex_m = [
        remote(
            ref.at[:, pl.ds(other, 256)],
            v.mw.at[k, pl.ds(pl.multiple_of(core * 64, 64), 64)],
            v.m_s.at[k],
            v.m_r.at[k],
            partner,
        )
        for k, ref in enumerate(moments)
    ]

    iota_h = lax.broadcasted_iota(jnp.int32, (NH, 128), 0)
    rate = jnp.zeros((NH, 128), F32)
    for h in range(NH):
        rate = jnp.where(iota_h == h, dr_s[h], rate)
    row = lax.broadcasted_iota(jnp.int32, (BLK, BLK), 0)
    col = lax.broadcasted_iota(jnp.int32, (BLK, BLK), 1)
    upper = (row <= col).astype(F32)
    rate2 = jnp.concatenate([rate, rate], axis=1)
    v.run[...] = jnp.zeros_like(v.run)
    ld_dt.wait()

    def pairs(lo, hi, body, before=None, after=None, carry=0):
        def trip(j, carry):
            two = (lo + 2 * j, lo + 2 * j + 1)
            if before is not None:
                for b in two:
                    before(b)
            for b in two:
                carry = body(b, carry)
            if after is not None:
                for b in two:
                    after(b)
            return carry

        return lax.fori_loop(0, (hi - lo) // 2, trip, carry)

    def hs(h):
        return slice(h * HD, (h + 1) * HD)

    logs = jnp.concatenate([-rate2 * v.dtv[:, b * BLK : (b + 1) * BLK] for b in range(NB)], axis=0)
    prefixes = lax.dot_general(
        logs, upper, (((1,), (0,)), ((), ())), precision=lax.Precision.HIGHEST, preferred_element_type=F32
    )
    v.pre[...] = prefixes.reshape(NB, NH, BLK)

    def a1(b, off):
        dt = v.dtv[:, pl.ds(pl.multiple_of(b * BLK, BLK), BLK)]
        prefix = v.pre[b]
        total = jnp.broadcast_to(prefix[:, BLK - 1 :], (NH, BLK))
        tail = jnp.exp(total - prefix)
        v.ep[b] = jnp.exp(prefix)
        v.e1[b] = jnp.exp(prefix - total)
        v.ecum[b] = jnp.exp(off + prefix)
        xt = v.xv[b].T
        v.xt[b] = xt
        for h in range(NH):
            scaled = (xt[hs(h)].astype(F32) * dt[h : h + 1]).astype(BF16)
            v.xa[b, hs(h)] = (scaled.astype(F32) * tail[h : h + 1]).astype(BF16)
        upd = nn(v.xa[b], v.bv[b])
        et = jnp.exp(total[:, :128])
        for h in range(NH):
            old = v.run[hs(h)]
            v.runs[b, hs(h)] = old.astype(BF16)
            v.run[hs(h)] = old * et[h : h + 1] + upd[hs(h)]
        return off + total

    ld_b.wait()
    dsum = pairs(0, NB, a1, before=lambda b: load_x(b).wait(), carry=jnp.zeros((NH, BLK), F32))
    v.ebuf[core] = v.run[...]
    v.dbuf[core] = dsum[:, :128]

    pl.semaphore_wait(barrier, 10)
    ex_e = [
        remote(v.ebuf.at[core], v.ebuf.at[core], v.e_s.at[0], v.e_r.at[0], partner),
        remote(v.dbuf.at[core], v.dbuf.at[core], v.e_s.at[1], v.e_r.at[1], partner),
    ]
    for cp in ex_e:
        cp.start()
    for cp in ex_m:
        cp.start()

    ld_c.wait()
    causal = row <= col

    def a2(b, carry):
        c_b = v.cv[b]
        scores = jnp.where(causal, nt(v.bv[b], c_b), 0.0).astype(BF16)
        local = nn(v.xa[b], scores)
        carried = nt(v.runs[b], c_b)
        for h in range(NH):
            v.acc[b, hs(h)] = local[hs(h)] * v.e1[b, h : h + 1] + carried[hs(h)] * v.ep[b, h : h + 1]
        zt = v.zv[b].T
        for h in range(NH):
            zz = zt[hs(h)].astype(F32)
            v.sil[b, hs(h)] = zz / (1.0 + jnp.exp(-zz))
        return carry

    pairs(0, 2, a2, before=lambda b: load_z(b).wait())

    for cp in ex_e:
        cp.wait()
    d0, d1 = v.dbuf[0], v.dbuf[1]
    v.dz[z] = d0 + d1
    dpre = jnp.where(core == 1, d0, 0.0)

    def hrow(ref, k, j):
        return jnp.exp(ref[k, pl.ds(core * 4 + j, 1)])

    for j in range(4):
        rows = pl.ds(pl.multiple_of(half + j * HD, HD), HD)
        v.sz[z, hs(j)] = (v.ebuf[0, rows] * hrow(v.dbuf, 1, j) + v.ebuf[1, rows]).astype(BF16)
    ex_z = []
    for d in range(3):
        ex_z.append(remote(v.sz.at[z], v.sz.at[z], v.z_s.at[d, 0], v.z_r.at[d, 0], zpeers[d]))
        ex_z.append(remote(v.dz.at[z], v.dz.at[z], v.z_s.at[d, 1], v.z_r.at[d, 1], zpeers[d]))
    for cp in ex_z:
        cp.start()
    pairs(2, 6, a2, before=lambda b: load_z(b).wait())

    for cp in ex_z:
        cp.wait()
    v.dy[y] = (v.dz[0] + v.dz[1]) + (v.dz[2] + v.dz[3])
    zpre = dpre
    for k in range(3):
        zpre = zpre + jnp.where(z > k, v.dz[k], 0.0)
    zflip = z + 1 - 2 * lax.rem(z, 2)
    for j in range(4):
        s01 = v.sz[0, hs(j)].astype(F32) * hrow(v.dz, 1, j) + v.sz[1, hs(j)].astype(F32)
        s012 = s01 * hrow(v.dz, 2, j) + v.sz[2, hs(j)].astype(F32)
        v.sy[y, hs(j)] = (s012 * hrow(v.dz, 3, j) + v.sz[3, hs(j)].astype(F32)).astype(BF16)
        rows = pl.ds(pl.multiple_of(half + j * HD, HD), HD)
        v.lev[1, rows] = v.sz[zflip, hs(j)]
        v.lev[2, rows] = s01.astype(BF16)
    ex_y = []
    for d in range(3):
        ex_y.append(remote(v.sy.at[y], v.sy.at[y], v.y_s.at[d, 0], v.y_r.at[d, 0], ypeers[d]))
        ex_y.append(remote(v.dy.at[y], v.dy.at[y], v.y_s.at[d, 1], v.y_r.at[d, 1], ypeers[d]))
    for cp in ex_y:
        cp.start()

    def swap(level):
        piece = v.lev.at[level, pl.ds(half, 256)]
        return remote(piece, piece, v.l_s.at[level - 1], v.l_r.at[level - 1], partner)

    for level in (1, 2):
        swap(level).start()
    v.lev[0] = v.ebuf[0].astype(BF16)

    def set_factor(level, value):
        v.fac[level] = jnp.concatenate([value, value], axis=1)

    set_factor(0, jnp.full((NH, 128), jnp.where(core == 1, 1.0, 0.0), F32))
    set_factor(1, jnp.where(lax.rem(z, 2) == 1, jnp.exp(dpre), 0.0))
    set_factor(2, jnp.where(z >= 2, jnp.exp(dpre + jnp.where(z == 3, v.dz[2], 0.0)), 0.0))
    pairs(6, 8, a2, before=lambda b: load_z(b).wait())
    ld_g.wait()
    for level in (1, 2):
        swap(level).wait()

    def scaled_gate(b, level):
        lanes = pl.ds(pl.multiple_of(b * BLK, BLK), BLK)
        return v.gatev[level, :, lanes] * (v.fac[level] * v.ecum[b])

    def b1(b, carry):
        c_b = v.cv[b]
        reads = [nt(v.lev[level], c_b) for level in range(3)]
        gates = [scaled_gate(b, level) for level in range(3)]
        for h in range(NH):
            add = reads[0][hs(h)] * gates[0][h : h + 1]
            for level in (1, 2):
                add = add + reads[level][hs(h)] * gates[level][h : h + 1]
            v.acc[b, hs(h)] = v.acc[b, hs(h)] + add
        return carry

    pairs(0, 6, b1)

    for cp in ex_y:
        cp.wait()
    yflip = y + 1 - 2 * lax.rem(y, 2)
    for j in range(4):
        s01 = v.sy[0, hs(j)].astype(F32) * hrow(v.dy, 1, j) + v.sy[1, hs(j)].astype(F32)
        rows = pl.ds(pl.multiple_of(half + j * HD, HD), HD)
        v.lev[3, rows] = v.sy[yflip, hs(j)]
        v.lev[4, rows] = s01.astype(BF16)
    for level in (3, 4):
        swap(level).start()
    set_factor(3, jnp.where(lax.rem(y, 2) == 1, jnp.exp(zpre), 0.0))
    set_factor(4, jnp.where(y >= 2, jnp.exp(zpre + jnp.where(y == 3, v.dy[2], 0.0)), 0.0))
    pairs(6, 8, b1)
    ld_n.wait()
    v.gcol[...] = jnp.broadcast_to(v.ngv[...], (128, CH)).T
    for level in (3, 4):
        swap(level).wait()

    def ex_q(b, d):
        piece = v.ssb.at[head, b]
        return remote(piece, piece, v.q_s.at[b, d], v.q_r.at[b, d], xpeers[d])

    def b2(b, carry):
        c_b = v.cv[b]
        reads = [nt(v.lev[level], c_b) for level in (3, 4)]
        gates = [scaled_gate(b, level) for level in (3, 4)]
        squares = jnp.zeros((8, BLK), F32)
        for h in range(NH):
            inside = v.acc[b, hs(h)] + reads[0][hs(h)] * gates[0][h : h + 1] + reads[1][hs(h)] * gates[1][h : h + 1]
            mixed = inside + v.xt[b, hs(h)].astype(F32) * sk_s[h]
            gated = mixed * v.sil[b, hs(h)]
            v.acc[b, hs(h)] = gated
            squares = squares + jnp.sum((gated * gated).reshape(8, 8, BLK), axis=0)
        v.ssb[head, b] = jnp.sum(squares, axis=0, keepdims=True)
        return carry

    def send_q(b):
        for d in range(3):
            ex_q(b, d).start()

    def wait_q(b):
        for d in range(3):
            ex_q(b, d).wait()

    def b3(b, carry):
        total = (v.ssb[0, b] + v.ssb[1, b]) + (v.ssb[2, b] + v.ssb[3, b])
        r = lax.rsqrt(total / INNER + 1e-05)
        lanes = pl.ds(pl.multiple_of(b * BLK, BLK), BLK)
        for h in range(NH):
            gain = v.gcol[hs(h)]
            n = v.acc[b, hs(h)] * r * jnp.concatenate([gain, gain], axis=1)
            v.nt_[hs(h), lanes] = n.astype(BF16)
        return carry

    def b4(b, carry):
        n_out[b] = v.nt_[:, pl.ds(pl.multiple_of(b * BLK, BLK), BLK)].T
        return carry

    pairs(0, NB, b2, after=send_q)
    pairs(0, NB, b3, before=wait_q)

    ld_cot.wait()
    def ex_p(p):
        return remote(v.gsend.at[p], v.grecv.at[p], v.p_s.at[p], v.p_r.at[p], partner)

    recv_bufs = (v.r0, v.r1, v.r2, v.r3)
    starts = (0, 8, 12, 14)

    def sent_masks(s, t):
        dims = stream_dims(s)
        return [m | (1 << dims[t]) for m in span(dims[t + 1 :])]

    def ex_r(s, t, i):
        dims = stream_dims(s)
        k = starts[t] + i
        return remote(v.sb.at[s, k], recv_bufs[t].at[s, i], v.r_s.at[s, k], v.r_r.at[s, k], cube[dims[t]])

    def finish_pair(p):
        ex_p(p).wait()
        for a in range(2):
            lanes = slice(a * 128, (a + 1) * 128)
            m = 2 * p + a
            total = v.gown[p, :, lanes] + v.grecv[p, :, lanes].astype(F32)
            for s in range(4):
                if m >> s & 1:
                    v.sb[s, sent_masks(s, 0).index(m)] = total[hs(s)].astype(BF16)
                else:
                    v.part[m, hs(s)] = total[hs(s)]
        for s in range(4):
            for i, m in enumerate(sent_masks(s, 0)):
                if m >> 1 == p:
                    ex_r(s, 0, i).start()

    def take(s, t, i):
        dims = stream_dims(s)
        m = span(dims[t + 1 :])[i]
        ex_r(s, t, i).wait()
        total = v.part[m, hs(s)] + recv_bufs[t][s, i].astype(F32)
        nxt = sent_masks(s, t + 1)
        if m in nxt:
            k = nxt.index(m)
            v.sb[s, starts[t + 1] + k] = total.astype(BF16)
            ex_r(s, t + 1, k).start()
        else:
            v.part[m, hs(s)] = total

    pending = schedule_events()

    def run_events(now):
        while pending and pending[0][0] <= now:
            take(*pending.pop(0)[1:])

    for p in range(7, -1, -1):
        sides = []
        for m in (2 * p, 2 * p + 1):
            yy, zz = flip(y, z, m)
            sides.append(v.cotv[:, pl.ds(pl.multiple_of((yy * 4 + zz) * 128, 128), 128)])
        cot = jnp.concatenate(sides, axis=1)
        v.gsend[p] = nn(v.nt_[pl.ds(other, 256), :], cot).astype(BF16)
        ex_p(p).start()
        v.gown[p] = nn(v.nt_[pl.ds(half, 256), :], cot)
        if p + LAG < 8:
            finish_pair(p + LAG)
            run_events(7 - p)
    for p in range(LAG - 1, -1, -1):
        finish_pair(p)
        run_events(7 - p + LAG)
    run_events(1000)
    for s in range(4):
        ex_r(s, 3, 0).wait()
        v.gt[:, hs(s)] = (v.part[0, hs(s)] + v.r3[s, 0].astype(F32)).T

    ex_g = remote(
        v.gt.at[pl.ds(pl.multiple_of((1 - core) * 64, 64), 64)], v.gx, v.g_s.at[0], v.g_r.at[0], partner
    )
    ex_g.start()
    for cp in ld_m:
        cp.wait()
    for cp in ex_m:
        cp.wait()
    own = y * 4 + z
    grad = v.gt[...]
    one = 0.9 * v.mw[1] + 0.1 * grad
    two = 0.95 * v.mw[2] + 0.05 * grad * grad
    ratio = one / (1.0 - 0.9**10) / (jnp.sqrt(two / (1.0 - 0.95**10)) + 1e-08)
    master = v.mw[0]
    v.w[own, core] = (master - 0.1 * (ratio + 0.1 * master)).astype(BF16)

    def slot(m):
        yy, zz = flip(y, z, m)
        return yy * 4 + zz

    def ex_a(s, t, i):
        dims = stream_dims(s)
        m = span(dims[:t])[i]
        piece = v.w.at[slot(m), core, pl.ds(s * 32, 32)]
        k = (1 << t) - 1 + i
        return remote(piece, piece, v.a_s.at[s, k], v.a_r.at[s, k], cube[dims[t]])

    def ex_c(s, i):
        m = span(stream_dims(s))[i]
        piece = v.w.at[slot(m), core, pl.ds(s * 32, 32)]
        return remote(piece, piece, v.c_s.at[s, i], v.c_r.at[s, i], partner)

    for t in range(4):
        for s in range(4):
            ex_a(s, t, 0).start()
    for s in range(4):
        ex_c(s, 0).start()
    lax.fori_loop(0, NB, b4, 0)
    for got in sorted(range(1, 16), key=lambda k: (bin(k).count("1"), k)):
        t = got.bit_length() - 1
        for s in range(4):
            ex_a(s, t, got - (1 << t)).wait_recv()
            for later in range(t + 1, 4):
                ex_a(s, later, got).start()
            ex_c(s, got).start()
    ex_g.wait()
    gt_out[...] = v.gt[pl.ds(pl.multiple_of(core * 64, 64), 64)]
    for s in range(4):
        for i in range(16):
            ex_c(s, i).wait()
    for s in range(4):
        for t in range(4):
            for i in range(1 << t):
                ex_a(s, t, i).wait_send()


def writer(n_v, w_v, gt_v, gx_v, n_out, w_out, g_out, sems):
    core = lax.rem(lax.axis_index("ctx"), 2)
    half = pl.multiple_of(core * 256, 256)
    other = pl.multiple_of((1 - core) * 256, 256)
    copies = [
        pltpu.make_async_copy(w_v.at[:, 0], w_out.at[:, :, pl.ds(0, 256)], sems.at[0]),
        pltpu.make_async_copy(w_v.at[:, 1], w_out.at[:, :, pl.ds(256, 256)], sems.at[1]),
        pltpu.make_async_copy(n_v, n_out, sems.at[2]),
        pltpu.make_async_copy(gt_v, g_out.at[:, pl.ds(half, 256)], sems.at[3]),
        pltpu.make_async_copy(gx_v, g_out.at[:, pl.ds(other, 256)], sems.at[4]),
    ]
    for cp in copies:
        cp.start()
    for cp in copies:
        cp.wait()


def on_device(
    entries, gating, state_in, state_out, step_size, decay_rate, skip_gain, level_gate,
    norm_gain, cotangent, master_weight, first_moment, second_moment,
):
    hbm = pl.BlockSpec(memory_space=pltpu.HBM)
    smem = pl.BlockSpec(memory_space=pltpu.SMEM)
    vmem = pl.BlockSpec(memory_space=pltpu.VMEM)
    parts = pl.pallas_call(
        kernel,
        out_shape=(
            pltpu.VMEM((NB, BLK, CH), BF16),
            pltpu.VMEM((16, 2, 128, 256), BF16),
            pltpu.VMEM((64, 256), F32),
            pltpu.VMEM((64, 256), F32),
        ),
        in_specs=[hbm] * 5 + [smem] * 2 + [hbm] * 6,
        out_specs=(vmem,) * 4,
        scratch_shapes=list(SCRATCH.values()),
        compiler_params=pltpu.CompilerParams(
            collective_id=0, has_side_effects=True, vmem_limit_bytes=59 * 1024 * 1024
        ),
    )(
        entries,
        gating,
        state_in.reshape(NB, BLK, ST),
        state_out.reshape(NB, BLK, ST),
        step_size,
        decay_rate,
        skip_gain,
        level_gate.transpose(1, 0, 2),
        norm_gain.reshape(1, CH),
        cotangent,
        master_weight,
        first_moment,
        second_moment,
    )
    normed, weights, gradient = pl.pallas_call(
        writer,
        out_shape=(
            jax.ShapeDtypeStruct((NB, BLK, CH), BF16),
            jax.ShapeDtypeStruct((16, 128, CH), BF16),
            jax.ShapeDtypeStruct((64, CH), F32),
        ),
        in_specs=[vmem] * 4,
        out_specs=(hbm,) * 3,
        scratch_shapes=[pltpu.SemaphoreType.DMA((5,))],
        compiler_params=pltpu.CompilerParams(vmem_limit_bytes=1024 * 1024),
    )(*parts)
    return normed.reshape(NB * BLK, CH), weights.reshape(DM, CH), gradient


def solution(mesh):
    return jax.shard_map(
        on_device,
        mesh=mesh,
        in_specs=(
            P("ctx", "head"),
            P("ctx", "head"),
            P("ctx", None),
            P("ctx", None),
            P("head", "ctx"),
            P("head"),
            P("head"),
            P("head", None, "ctx"),
            P("head"),
            P("ctx", None),
            P("ctx", "head"),
            P("ctx", "head"),
            P("ctx", "head"),
        ),
        out_specs=(P("ctx", "head"), P(None, "head"), P("ctx", "head")),
        check_vma=False,
    )
```

```python
import jax
import jax.numpy as jnp
from jax import lax
from jax.experimental import pallas as pl
from jax.experimental.pallas import tpu as pltpu
from jax.sharding import PartitionSpec as P

HD = 64
BLK = 256
NB = 8
NH = 8
CH = 512
ST = 128
LEV = 5
INNER = 2048
DM = 2048
F32 = jnp.float32
BF16 = jnp.bfloat16
MESH = pl.DeviceIdType.MESH
DIMS = 4


def nt(a, b):
    return lax.dot_general(a, b, (((1,), (1,)), ((), ())), preferred_element_type=F32)


def nn(a, b):
    return lax.dot_general(a, b, (((1,), (0,)), ((), ())), preferred_element_type=F32)


def flip(y, z, mask):
    if mask & 1:
        z = z + 1 - 2 * lax.rem(z, 2)
    if mask & 2:
        z = 3 - z
    if mask & 4:
        y = y + 1 - 2 * lax.rem(y, 2)
    if mask & 8:
        y = 3 - y
    return y, z


def stream_dims(s):
    return [((0, 2, 1, 3)[s] + t) % DIMS for t in range(DIMS)]


def span(dims):
    masks = [0]
    for d in dims:
        masks = masks + [m | (1 << d) for m in masks]
    return masks


LAG = 4
HOP = 6
UPDATE = 2


def group_of(s):
    return s // 2


def schedule():
    out = []
    ready = [0, 0]
    for s in range(4):
        dims = stream_dims(s)
        done = {m: 8 * group_of(s) + 7 - (m >> 1) + LAG for m in range(16)}
        sent = {m: done[m] for m in range(16) if m >> dims[0] & 1}
        for t in range(4):
            for i, m in enumerate(span(dims[t + 1 :])):
                when = max(sent[m | 1 << dims[t]] + HOP, done[m])
                done[m] = when
                out.append((when, 0, t, i, s))
                if t < 3 and m >> dims[t + 1] & 1:
                    sent[m] = when
        ready[group_of(s)] = max(ready[group_of(s)], done[0])
    for g in range(2):
        out.append((ready[g], 1, g))
        for got in range(1, 16):
            hops = bin(got).count("1")
            for s in (2 * g, 2 * g + 1):
                out.append((ready[g] + UPDATE + HOP * hops, 2, got, s))
    return sorted(out)


SCRATCH = dict(
    xv=pltpu.VMEM((NB, BLK, CH), BF16),
    pre=pltpu.VMEM((NB, NH, BLK), F32),
    zv=pltpu.VMEM((NB, BLK, CH), BF16),
    bv=pltpu.VMEM((NB, BLK, ST), BF16),
    cv=pltpu.VMEM((NB, BLK, ST), BF16),
    dtv=pltpu.VMEM((NH, NB * BLK), F32),
    gatev=pltpu.VMEM((LEV, NH, NB * BLK), F32),
    ngv=pltpu.VMEM((1, CH), F32),
    gcol=pltpu.VMEM((CH, 128), F32),
    xt=pltpu.VMEM((NB, CH, BLK), BF16),
    xa=pltpu.VMEM((NB, CH, BLK), BF16),
    runs=pltpu.VMEM((NB, CH, ST), BF16),
    run=pltpu.VMEM((CH, ST), F32),
    acc=pltpu.VMEM((NB, CH, BLK), F32),
    sil=pltpu.VMEM((NB, CH, BLK), F32),
    ep=pltpu.VMEM((NB, NH, BLK), F32),
    e1=pltpu.VMEM((NB, NH, BLK), F32),
    ecum=pltpu.VMEM((NB, NH, BLK), F32),
    ebuf=pltpu.VMEM((2, CH, ST), BF16),
    dbuf=pltpu.VMEM((2, NH, 128), F32),
    sz=pltpu.VMEM((4, CH // 2, ST), BF16),
    dz=pltpu.VMEM((4, NH, 128), F32),
    sy=pltpu.VMEM((4, CH // 2, ST), BF16),
    dy=pltpu.VMEM((4, NH, 128), F32),
    lev=pltpu.VMEM((LEV, CH, ST), BF16),
    fac=pltpu.VMEM((LEV, NH, BLK), F32),
    ssb=pltpu.VMEM((4, NB, 1, BLK), F32),
    nt_=pltpu.VMEM((CH, NB * BLK), BF16),
    cotv=pltpu.VMEM((NB * BLK, DM), BF16),
    gsend=pltpu.VMEM((2, 8, 128, 256), BF16),
    gown=pltpu.VMEM((2, 8, 128, 256), F32),
    grecv=pltpu.VMEM((2, 8, 128, 256), BF16),
    part=pltpu.VMEM((16, 256, 128), F32),
    sb=pltpu.VMEM((4, 15, HD, 128), BF16),
    r0=pltpu.VMEM((4, 8, HD, 128), BF16),
    r1=pltpu.VMEM((4, 4, HD, 128), BF16),
    r2=pltpu.VMEM((4, 2, HD, 128), BF16),
    r3=pltpu.VMEM((4, 1, HD, 128), BF16),
    gt=pltpu.VMEM((128, 256), F32),
    mw=pltpu.VMEM((3, 128, 256), F32),
    s_x=pltpu.SemaphoreType.DMA((NB,)),
    s_z=pltpu.SemaphoreType.DMA((NB,)),
    s_in=pltpu.SemaphoreType.DMA((6,)),
    s_m=pltpu.SemaphoreType.DMA((3,)),
    e_s=pltpu.SemaphoreType.DMA((3,)),
    e_r=pltpu.SemaphoreType.DMA((3,)),
    z_s=pltpu.SemaphoreType.DMA((3, 2)),
    z_r=pltpu.SemaphoreType.DMA((3, 2)),
    y_s=pltpu.SemaphoreType.DMA((3, 2)),
    y_r=pltpu.SemaphoreType.DMA((3, 2)),
    l_s=pltpu.SemaphoreType.DMA((4,)),
    l_r=pltpu.SemaphoreType.DMA((4,)),
    q_s=pltpu.SemaphoreType.DMA((NB, 3)),
    q_r=pltpu.SemaphoreType.DMA((NB, 3)),
    m_s=pltpu.SemaphoreType.DMA((3,)),
    m_r=pltpu.SemaphoreType.DMA((3,)),
    p_s=pltpu.SemaphoreType.DMA((2, 8)),
    p_r=pltpu.SemaphoreType.DMA((2, 8)),
    r_s=pltpu.SemaphoreType.DMA((4, 15)),
    r_r=pltpu.SemaphoreType.DMA((4, 15)),
    g_s=pltpu.SemaphoreType.DMA((1,)),
    g_r=pltpu.SemaphoreType.DMA((1,)),
    a_s=pltpu.SemaphoreType.DMA((4, 15)),
    a_r=pltpu.SemaphoreType.DMA((4, 15)),
    c_s=pltpu.SemaphoreType.DMA((4, 16)),
    c_r=pltpu.SemaphoreType.DMA((4, 16)),
)


class Refs:
    pass


def kernel(
    x_h, z_h, b_h, c_h, dt_h, dr_s, sk_s, gate_h, ng_h, cot_h, mw_h, m1_h, m2_h,
    n_out, w_out, gt_out, gx_out, *scratch,
):
    v = Refs()
    for name, ref in zip(SCRATCH, scratch):
        setattr(v, name, ref)
    v.w, v.gx = w_out, gx_out
    ctx = lax.axis_index("ctx")
    head = lax.axis_index("head")
    core = lax.rem(ctx, 2)
    z = lax.rem(ctx // 2, 4)
    y = ctx // 8
    half = pl.multiple_of(core * 256, 256)
    other = pl.multiple_of((1 - core) * 256, 256)

    def at(yy, zz, cc):
        return ((yy * 4 + zz) * 2 + cc, head)

    partner = at(y, z, 1 - core)
    zpeers = [at(y, lax.rem(z + d, 4), core) for d in (1, 2, 3)]
    ypeers = [at(lax.rem(y + d, 4), z, core) for d in (1, 2, 3)]
    xpeers = [(ctx, lax.rem(head + d, 4)) for d in (1, 2, 3)]
    cube = []
    for d in range(DIMS):
        yy, zz = flip(y, z, 1 << d)
        cube.append(at(yy, zz, core))

    def remote(src, dst, ssem, rsem, dev):
        return pltpu.make_async_remote_copy(
            src_ref=src, dst_ref=dst, send_sem=ssem, recv_sem=rsem, device_id=dev, device_id_type=MESH
        )

    barrier = pltpu.get_barrier_semaphore()
    for dev in [partner] + zpeers + ypeers + xpeers:
        pl.semaphore_signal(barrier, inc=1, device_id=dev, device_id_type=MESH)

    def load_x(b):
        return pltpu.make_async_copy(x_h.at[pl.ds(b * BLK, BLK)], v.xv.at[b], v.s_x.at[b])

    def load_z(b):
        return pltpu.make_async_copy(z_h.at[pl.ds(b * BLK, BLK)], v.zv.at[b], v.s_z.at[b])

    ld_dt = pltpu.make_async_copy(dt_h, v.dtv, v.s_in.at[0])
    ld_b = pltpu.make_async_copy(b_h, v.bv, v.s_in.at[1])
    ld_c = pltpu.make_async_copy(c_h, v.cv, v.s_in.at[2])
    ld_g = pltpu.make_async_copy(gate_h, v.gatev, v.s_in.at[3])
    ld_n = pltpu.make_async_copy(ng_h, v.ngv, v.s_in.at[4])
    ld_cot = pltpu.make_async_copy(cot_h, v.cotv, v.s_in.at[5])
    ld_dt.start()
    load_x(0).start()
    ld_b.start()
    for b in range(1, NB):
        load_x(b).start()
    ld_c.start()
    for b in range(NB):
        load_z(b).start()
    ld_g.start()
    ld_n.start()
    ld_cot.start()
    moments = (mw_h, m1_h, m2_h)
    ld_m = [
        pltpu.make_async_copy(
            ref.at[:, pl.ds(half, 256)],
            v.mw.at[k, pl.ds(pl.multiple_of(core * 64, 64), 64)],
            v.s_m.at[k],
        )
        for k, ref in enumerate(moments)
    ]
    for cp in ld_m:
        cp.start()
    ex_m = [
        remote(
            ref.at[:, pl.ds(other, 256)],
            v.mw.at[k, pl.ds(pl.multiple_of(core * 64, 64), 64)],
            v.m_s.at[k],
            v.m_r.at[k],
            partner,
        )
        for k, ref in enumerate(moments)
    ]

    iota_h = lax.broadcasted_iota(jnp.int32, (NH, 128), 0)
    rate = jnp.zeros((NH, 128), F32)
    for h in range(NH):
        rate = jnp.where(iota_h == h, dr_s[h], rate)
    row = lax.broadcasted_iota(jnp.int32, (BLK, BLK), 0)
    col = lax.broadcasted_iota(jnp.int32, (BLK, BLK), 1)
    upper = (row <= col).astype(F32)
    rate2 = jnp.concatenate([rate, rate], axis=1)
    v.run[...] = jnp.zeros_like(v.run)
    ld_dt.wait()

    def pairs(lo, hi, body, before=None, after=None, carry=0):
        def trip(j, carry):
            two = (lo + 2 * j, lo + 2 * j + 1)
            if before is not None:
                for b in two:
                    before(b)
            for b in two:
                carry = body(b, carry)
            if after is not None:
                for b in two:
                    after(b)
            return carry

        return lax.fori_loop(0, (hi - lo) // 2, trip, carry)

    def hs(h):
        return slice(h * HD, (h + 1) * HD)

    logs = jnp.concatenate([-rate2 * v.dtv[:, b * BLK : (b + 1) * BLK] for b in range(NB)], axis=0)
    prefixes = lax.dot_general(
        logs, upper, (((1,), (0,)), ((), ())), precision=lax.Precision.HIGHEST, preferred_element_type=F32
    )
    v.pre[...] = prefixes.reshape(NB, NH, BLK)

    def a1(b, off):
        dt = v.dtv[:, pl.ds(pl.multiple_of(b * BLK, BLK), BLK)]
        prefix = v.pre[b]
        total = jnp.broadcast_to(prefix[:, BLK - 1 :], (NH, BLK))
        tail = jnp.exp(total - prefix)
        v.ep[b] = jnp.exp(prefix)
        v.e1[b] = jnp.exp(prefix - total)
        v.ecum[b] = jnp.exp(off + prefix)
        xt = v.xv[b].T
        v.xt[b] = xt
        for h in range(NH):
            scaled = (xt[hs(h)].astype(F32) * dt[h : h + 1]).astype(BF16)
            v.xa[b, hs(h)] = (scaled.astype(F32) * tail[h : h + 1]).astype(BF16)
        upd = nn(v.xa[b], v.bv[b])
        et = jnp.exp(total[:, :128])
        for h in range(NH):
            old = v.run[hs(h)]
            v.runs[b, hs(h)] = old.astype(BF16)
            v.run[hs(h)] = old * et[h : h + 1] + upd[hs(h)]
        return off + total

    ld_b.wait()
    dsum = pairs(0, NB, a1, before=lambda b: load_x(b).wait(), carry=jnp.zeros((NH, BLK), F32))
    v.ebuf[core] = v.run[...].astype(BF16)
    v.dbuf[core] = dsum[:, :128]

    pl.semaphore_wait(barrier, 10)
    first, rest = v.ebuf.at[core, pl.ds(other, 256)], v.ebuf.at[core, pl.ds(half, 256)]
    ex_e = [
        remote(v.dbuf.at[core], v.dbuf.at[core], v.e_s.at[1], v.e_r.at[1], partner),
        remote(first, first, v.e_s.at[0], v.e_r.at[0], partner),
        remote(rest, rest, v.e_s.at[2], v.e_r.at[2], partner),
    ]
    for cp in ex_e:
        cp.start()
    for cp in ex_m:
        cp.start()

    ld_c.wait()
    causal = row <= col

    def a2(b, carry):
        c_b = v.cv[b]
        scores = jnp.where(causal, nt(v.bv[b], c_b), 0.0).astype(BF16)
        local = nn(v.xa[b], scores)
        carried = nt(v.runs[b], c_b)
        for h in range(NH):
            v.acc[b, hs(h)] = local[hs(h)] * v.e1[b, h : h + 1] + carried[hs(h)] * v.ep[b, h : h + 1]
        zt = v.zv[b].T
        for h in range(NH):
            zz = zt[hs(h)].astype(F32)
            v.sil[b, hs(h)] = zz / (1.0 + jnp.exp(-zz))
        return carry

    pairs(0, 2, a2, before=lambda b: load_z(b).wait())

    for cp in ex_e[:2]:
        cp.wait()
    d0, d1 = v.dbuf[0], v.dbuf[1]
    v.dz[z] = d0 + d1
    dpre = jnp.where(core == 1, d0, 0.0)

    def hrow(ref, k, j):
        return jnp.exp(ref[k, pl.ds(core * 4 + j, 1)])

    for j in range(4):
        rows = pl.ds(pl.multiple_of(half + j * HD, HD), HD)
        v.sz[z, hs(j)] = (
            v.ebuf[0, rows].astype(F32) * hrow(v.dbuf, 1, j) + v.ebuf[1, rows].astype(F32)
        ).astype(BF16)
    ex_z = []
    for d in range(3):
        ex_z.append(remote(v.sz.at[z], v.sz.at[z], v.z_s.at[d, 0], v.z_r.at[d, 0], zpeers[d]))
        ex_z.append(remote(v.dz.at[z], v.dz.at[z], v.z_s.at[d, 1], v.z_r.at[d, 1], zpeers[d]))
    for cp in ex_z:
        cp.start()
    pairs(2, 6, a2, before=lambda b: load_z(b).wait())

    for cp in ex_z:
        cp.wait()
    v.dy[y] = (v.dz[0] + v.dz[1]) + (v.dz[2] + v.dz[3])
    zpre = dpre
    for k in range(3):
        zpre = zpre + jnp.where(z > k, v.dz[k], 0.0)
    zflip = z + 1 - 2 * lax.rem(z, 2)
    for j in range(4):
        s01 = v.sz[0, hs(j)].astype(F32) * hrow(v.dz, 1, j) + v.sz[1, hs(j)].astype(F32)
        s012 = s01 * hrow(v.dz, 2, j) + v.sz[2, hs(j)].astype(F32)
        v.sy[y, hs(j)] = (s012 * hrow(v.dz, 3, j) + v.sz[3, hs(j)].astype(F32)).astype(BF16)
        rows = pl.ds(pl.multiple_of(half + j * HD, HD), HD)
        v.lev[1, rows] = v.sz[zflip, hs(j)]
        v.lev[2, rows] = s01.astype(BF16)
    ex_y = []
    for d in range(3):
        ex_y.append(remote(v.sy.at[y], v.sy.at[y], v.y_s.at[d, 0], v.y_r.at[d, 0], ypeers[d]))
        ex_y.append(remote(v.dy.at[y], v.dy.at[y], v.y_s.at[d, 1], v.y_r.at[d, 1], ypeers[d]))
    for cp in ex_y:
        cp.start()

    def swap(level):
        piece = v.lev.at[level, pl.ds(half, 256)]
        return remote(piece, piece, v.l_s.at[level - 1], v.l_r.at[level - 1], partner)

    for level in (1, 2):
        swap(level).start()
    ex_e[2].wait()
    v.lev[0] = v.ebuf[0]

    def set_factor(level, value):
        v.fac[level] = jnp.concatenate([value, value], axis=1)

    set_factor(0, jnp.full((NH, 128), jnp.where(core == 1, 1.0, 0.0), F32))
    set_factor(1, jnp.where(lax.rem(z, 2) == 1, jnp.exp(dpre), 0.0))
    set_factor(2, jnp.where(z >= 2, jnp.exp(dpre + jnp.where(z == 3, v.dz[2], 0.0)), 0.0))
    pairs(6, 8, a2, before=lambda b: load_z(b).wait())
    ld_g.wait()
    for level in (1, 2):
        swap(level).wait()

    def scaled_gate(b, level):
        lanes = pl.ds(pl.multiple_of(b * BLK, BLK), BLK)
        return v.gatev[level, :, lanes] * (v.fac[level] * v.ecum[b])

    def b1(b, carry):
        c_b = v.cv[b]
        reads = [nt(v.lev[level], c_b) for level in range(3)]
        gates = [scaled_gate(b, level) for level in range(3)]
        for h in range(NH):
            add = reads[0][hs(h)] * gates[0][h : h + 1]
            for level in (1, 2):
                add = add + reads[level][hs(h)] * gates[level][h : h + 1]
            v.acc[b, hs(h)] = v.acc[b, hs(h)] + add
        return carry

    pairs(0, 6, b1)

    for cp in ex_y:
        cp.wait()
    yflip = y + 1 - 2 * lax.rem(y, 2)
    for j in range(4):
        s01 = v.sy[0, hs(j)].astype(F32) * hrow(v.dy, 1, j) + v.sy[1, hs(j)].astype(F32)
        rows = pl.ds(pl.multiple_of(half + j * HD, HD), HD)
        v.lev[3, rows] = v.sy[yflip, hs(j)]
        v.lev[4, rows] = s01.astype(BF16)
    for level in (3, 4):
        swap(level).start()
    set_factor(3, jnp.where(lax.rem(y, 2) == 1, jnp.exp(zpre), 0.0))
    set_factor(4, jnp.where(y >= 2, jnp.exp(zpre + jnp.where(y == 3, v.dy[2], 0.0)), 0.0))
    pairs(6, 8, b1)
    ld_n.wait()
    v.gcol[...] = jnp.broadcast_to(v.ngv[...], (128, CH)).T
    for level in (3, 4):
        swap(level).wait()

    def ex_q(b, d):
        piece = v.ssb.at[head, b]
        return remote(piece, piece, v.q_s.at[b, d], v.q_r.at[b, d], xpeers[d])

    def b2(b, carry):
        c_b = v.cv[b]
        reads = [nt(v.lev[level], c_b) for level in (3, 4)]
        gates = [scaled_gate(b, level) for level in (3, 4)]
        squares = jnp.zeros((8, BLK), F32)
        for h in range(NH):
            inside = v.acc[b, hs(h)] + reads[0][hs(h)] * gates[0][h : h + 1] + reads[1][hs(h)] * gates[1][h : h + 1]
            mixed = inside + v.xt[b, hs(h)].astype(F32) * sk_s[h]
            gated = mixed * v.sil[b, hs(h)]
            v.acc[b, hs(h)] = gated
            squares = squares + jnp.sum((gated * gated).reshape(8, 8, BLK), axis=0)
        v.ssb[head, b] = jnp.sum(squares, axis=0, keepdims=True)
        return carry

    def send_q(b):
        for d in range(3):
            ex_q(b, d).start()

    def wait_q(b):
        for d in range(3):
            ex_q(b, d).wait()

    def b3(b, carry):
        total = (v.ssb[0, b] + v.ssb[1, b]) + (v.ssb[2, b] + v.ssb[3, b])
        r = lax.rsqrt(total / INNER + 1e-05)
        lanes = pl.ds(pl.multiple_of(b * BLK, BLK), BLK)
        for h in range(NH):
            gain = v.gcol[hs(h)]
            n = v.acc[b, hs(h)] * r * jnp.concatenate([gain, gain], axis=1)
            v.nt_[hs(h), lanes] = n.astype(BF16)
        return carry

    def b4(b, carry):
        n_out[b] = v.nt_[:, pl.ds(pl.multiple_of(b * BLK, BLK), BLK)].T
        return carry

    pairs(0, NB, b2, after=send_q)
    pairs(0, NB, b3, before=wait_q)

    ld_cot.wait()
    def ex_p(g, p):
        return remote(v.gsend.at[g, p], v.grecv.at[g, p], v.p_s.at[g, p], v.p_r.at[g, p], partner)

    recv_bufs = (v.r0, v.r1, v.r2, v.r3)
    starts = (0, 8, 12, 14)

    def sent_masks(s, t):
        dims = stream_dims(s)
        return [m | (1 << dims[t]) for m in span(dims[t + 1 :])]

    def ex_r(s, t, i):
        dims = stream_dims(s)
        k = starts[t] + i
        return remote(v.sb.at[s, k], recv_bufs[t].at[s, i], v.r_s.at[s, k], v.r_r.at[s, k], cube[dims[t]])

    def finish_pair(g, p):
        ex_p(g, p).wait()
        streams = (2 * g, 2 * g + 1)
        for a in range(2):
            lanes = slice(a * 128, (a + 1) * 128)
            m = 2 * p + a
            total = v.gown[g, p, :, lanes] + v.grecv[g, p, :, lanes].astype(F32)
            for s in streams:
                rows = total[hs(s % 2)]
                if m >> stream_dims(s)[0] & 1:
                    v.sb[s, sent_masks(s, 0).index(m)] = rows.astype(BF16)
                else:
                    v.part[m, hs(s)] = rows
        for s in streams:
            for i, m in enumerate(sent_masks(s, 0)):
                if m >> 1 == p:
                    ex_r(s, 0, i).start()

    def take(t, i, s):
        dims = stream_dims(s)
        m = span(dims[t + 1 :])[i]
        ex_r(s, t, i).wait()
        total = v.part[m, hs(s)] + recv_bufs[t][s, i].astype(F32)
        nxt = sent_masks(s, t + 1) if t < 3 else []
        if m in nxt:
            k = nxt.index(m)
            v.sb[s, starts[t + 1] + k] = total.astype(BF16)
            ex_r(s, t + 1, k).start()
        else:
            v.part[m, hs(s)] = total

    own = y * 4 + z

    def update(g):
        cols = slice(g * 128, (g + 1) * 128)
        grad = v.part[0, cols].T
        v.gt[:, cols] = grad
        one = 0.9 * v.mw[1, :, cols] + 0.1 * grad
        two = 0.95 * v.mw[2, :, cols] + 0.05 * grad * grad
        ratio = one / (1.0 - 0.9**10) / (jnp.sqrt(two / (1.0 - 0.95**10)) + 1e-08)
        master = v.mw[0, :, cols]
        v.w[own, core, g] = (master - 0.1 * (ratio + 0.1 * master)).astype(BF16)
        for t in range(4):
            for s in (2 * g, 2 * g + 1):
                ex_a(s, t, 0).start()
        for s in (2 * g, 2 * g + 1):
            ex_c(s, 0).start()

    def slot(m):
        yy, zz = flip(y, z, m)
        return yy * 4 + zz

    def piece_of(s, m):
        return v.w.at[slot(m), core, group_of(s), pl.ds(s % 2 * 64, 64)]

    def ex_a(s, t, i):
        dims = stream_dims(s)
        piece = piece_of(s, span(dims[:t])[i])
        k = (1 << t) - 1 + i
        return remote(piece, piece, v.a_s.at[s, k], v.a_r.at[s, k], cube[dims[t]])

    def ex_c(s, i):
        piece = piece_of(s, span(stream_dims(s))[i])
        return remote(piece, piece, v.c_s.at[s, i], v.c_r.at[s, i], partner)

    def forward(got, s):
        t = got.bit_length() - 1
        ex_a(s, t, got - (1 << t)).wait_recv()
        for later in range(t + 1, 4):
            ex_a(s, later, got).start()
        ex_c(s, got).start()

    pending = schedule()

    def run_events(now):
        while pending and pending[0][0] <= now:
            (take, update, forward)[pending[0][1]](*pending.pop(0)[2:])

    for cp in ld_m:
        cp.wait()
    for cp in ex_m:
        cp.wait()
    products = [(g, p) for g in range(2) for p in range(7, -1, -1)]
    for step in range(len(products) + LAG):
        if step < len(products):
            g, p = products[step]
            sides = []
            for m in (2 * p, 2 * p + 1):
                yy, zz = flip(y, z, m)
                sides.append(v.cotv[:, pl.ds(pl.multiple_of((yy * 4 + zz) * 128, 128), 128)])
            rows = [v.nt_[pl.ds(pl.multiple_of(side + g * 128, 128), 128), :] for side in (other, half)]
            product = nn(jnp.concatenate(rows, axis=0), jnp.concatenate(sides, axis=1))
            v.gsend[g, p] = product[:128].astype(BF16)
            ex_p(g, p).start()
            v.gown[g, p] = product[128:]
        if step >= LAG:
            finish_pair(*products[step - LAG])
            run_events(step)
    lax.fori_loop(0, NB, b4, 0)
    run_events(10000)

    ex_g = remote(
        v.gt.at[pl.ds(pl.multiple_of((1 - core) * 64, 64), 64)], v.gx, v.g_s.at[0], v.g_r.at[0], partner
    )
    ex_g.start()
    gt_out[...] = v.gt[pl.ds(pl.multiple_of(core * 64, 64), 64)]
    ex_g.wait()
    for s in range(4):
        for i in range(16):
            ex_c(s, i).wait()
    for s in range(4):
        for t in range(4):
            for i in range(1 << t):
                ex_a(s, t, i).wait_send()


def writer(n_v, w_v, gt_v, gx_v, n_out, w_out, g_out, sems):
    core = lax.rem(lax.axis_index("ctx"), 2)
    half = pl.multiple_of(core * 256, 256)
    other = pl.multiple_of((1 - core) * 256, 256)
    copies = [
        pltpu.make_async_copy(w_v.at[:, k // 2, k % 2], w_out.at[:, :, pl.ds(k * 128, 128)], sems.at[k])
        for k in range(4)
    ]
    copies += [
        pltpu.make_async_copy(n_v.at[pl.ds(k * 2, 2)], n_out.at[pl.ds(k * 2, 2)], sems.at[4 + k]) for k in range(4)
    ]
    copies += [
        pltpu.make_async_copy(gt_v, g_out.at[:, pl.ds(half, 256)], sems.at[8]),
        pltpu.make_async_copy(gx_v, g_out.at[:, pl.ds(other, 256)], sems.at[9]),
    ]
    for cp in copies:
        cp.start()
    for cp in copies:
        cp.wait()


def on_device(
    entries, gating, state_in, state_out, step_size, decay_rate, skip_gain, level_gate,
    norm_gain, cotangent, master_weight, first_moment, second_moment,
):
    hbm = pl.BlockSpec(memory_space=pltpu.HBM)
    smem = pl.BlockSpec(memory_space=pltpu.SMEM)
    vmem = pl.BlockSpec(memory_space=pltpu.VMEM)
    parts = pl.pallas_call(
        kernel,
        out_shape=(
            pltpu.VMEM((NB, BLK, CH), BF16),
            pltpu.VMEM((16, 2, 2, 128, 128), BF16),
            pltpu.VMEM((64, 256), F32),
            pltpu.VMEM((64, 256), F32),
        ),
        in_specs=[hbm] * 5 + [smem] * 2 + [hbm] * 6,
        out_specs=(vmem,) * 4,
        scratch_shapes=list(SCRATCH.values()),
        compiler_params=pltpu.CompilerParams(
            collective_id=0, has_side_effects=True, vmem_limit_bytes=59 * 1024 * 1024
        ),
    )(
        entries,
        gating,
        state_in.reshape(NB, BLK, ST),
        state_out.reshape(NB, BLK, ST),
        step_size,
        decay_rate,
        skip_gain,
        level_gate.transpose(1, 0, 2),
        norm_gain.reshape(1, CH),
        cotangent,
        master_weight,
        first_moment,
        second_moment,
    )
    normed, weights, gradient = pl.pallas_call(
        writer,
        out_shape=(
            jax.ShapeDtypeStruct((NB, BLK, CH), BF16),
            jax.ShapeDtypeStruct((16, 128, CH), BF16),
            jax.ShapeDtypeStruct((64, CH), F32),
        ),
        in_specs=[vmem] * 4,
        out_specs=(hbm,) * 3,
        scratch_shapes=[pltpu.SemaphoreType.DMA((10,))],
        compiler_params=pltpu.CompilerParams(vmem_limit_bytes=1024 * 1024),
    )(*parts)
    return normed.reshape(NB * BLK, CH), weights.reshape(DM, CH), gradient


def solution(mesh):
    return jax.shard_map(
        on_device,
        mesh=mesh,
        in_specs=(
            P("ctx", "head"),
            P("ctx", "head"),
            P("ctx", None),
            P("ctx", None),
            P("head", "ctx"),
            P("head"),
            P("head"),
            P("head", None, "ctx"),
            P("head"),
            P("ctx", None),
            P("ctx", "head"),
            P("ctx", "head"),
            P("ctx", "head"),
        ),
        out_specs=(P("ctx", "head"), P(None, "head"), P("ctx", "head")),
        check_vma=False,
    )
```
